32 devices in a mesh: depth: 16 (over z, y, x), rows: 2 (over core).
Axes of the slice: x: 2, y: 2, z: 4, core: 2. Of those that a mesh axis runs over, the one named last changes fastest.
Arguments:
- field: bfloat16 [256, 128, 1024], P('depth', 'rows'), may hold values from -6 to 6
- tf_centers: float32 [4], replicated, may hold values from -1.5 to 1.5
- tf_widths: float32 [4], replicated, may hold values from 0.4 to 1.2
- tf_density: float32 [4], replicated, may hold values from 0.5 to 4
- tf_colors: float32 [3, 4], replicated, may hold values from 0.1 to 1
- light: float32 [3], replicated, may hold values from 0.5 to 1.5
Outputs:
- image: float32 [4, 128, 1024], P(None, 'rows', 'depth')
The draws below stay inside these ranges and needn't reach their ends.
All inputs are finite; a program needn't handle non-finite values.
Results may differ from the reference program's by a relative error of at most 0.0003.
Values may be sent and summed in bfloat16 or wider, within the bound.
A program may use at most 64 MiB of HBM per device.

```python
import math
import jax
import jax.numpy as jnp
from jax import lax

YD = 64
NX = 1024
BUMPS = 4
NZ = 256
NY = 128


def steps_of(rng, shape, cuts, smallest, largest):
    def one(dim, shards_of):
        heights = jax.random.uniform(jax.random.fold_in(jax.random.fold_in(rng, 6), dim), (shards_of,), jnp.float32, smallest / len(cuts), largest / len(cuts))
        return jnp.repeat(jnp.exp(heights), shape[dim] // shards_of).reshape((-1,) + (1,) * (len(shape) - dim - 1))

    loudness = one(*cuts[0])
    for cut in cuts[1:]:
        loudness = loudness * one(*cut)
    return loudness


def normal_values(own_key, shape, spread, bound, shards=(), kind=jnp.bfloat16):
    level = steps_of(own_key, shape, shards, -0.22, 0.18) if shards else 1.0
    values = jax.random.normal(own_key, shape, jnp.float32) * spread * level
    return jnp.minimum(jnp.maximum(values, -bound), bound).astype(kind)


def setup_inputs(seed: int = 0) -> dict:
    key_list = jax.random.split(jax.random.key(seed), 7)
    field = normal_values(key_list[0], (NZ, NY, NX), 1.0, 6.0, ((0, 16), (1, 2)))
    tf_centers = jnp.clip(jax.random.uniform(key_list[1], (BUMPS,), jnp.float32, -1.5, 1.5), -1.5, 1.5)
    tf_widths = jnp.clip(jnp.exp(jax.random.uniform(key_list[2], (BUMPS,), jnp.float32, math.log(0.4), math.log(1.2))), 0.4, 1.2)
    tf_density = jnp.clip(jnp.exp(jax.random.uniform(key_list[3], (BUMPS,), jnp.float32, math.log(0.5), math.log(4.0))), 0.5, 4.0)
    tf_colors = jnp.clip(jax.random.uniform(key_list[4], (3, BUMPS), jnp.float32, 0.1, 1.0), 0.1, 1.0)
    light = jnp.clip(jax.random.uniform(key_list[5], (3,), jnp.float32, 0.5, 1.5), 0.5, 1.5)
    return {"field": field, "tf_centers": tf_centers, "tf_widths": tf_widths, "tf_density": tf_density, "tf_colors": tf_colors, "light": light}


def shade_cells(padded, tf_centers, tf_widths, tf_density, tf_colors, light, step_size):
    values = padded[1:-1, 1:-1, 1:-1]
    grad_z = (padded[2:, 1:-1, 1:-1] - padded[:-2, 1:-1, 1:-1]) * 0.5
    grad_y = (padded[1:-1, 2:, 1:-1] - padded[1:-1, :-2, 1:-1]) * 0.5
    grad_x = (padded[1:-1, 1:-1, 2:] - padded[1:-1, 1:-1, :-2]) * 0.5
    grad_sq = grad_z * grad_z + grad_y * grad_y + grad_x * grad_x
    light_dir = light / jnp.sqrt(jnp.sum(light * light))
    facing = jnp.abs(grad_z * light_dir[0] + grad_y * light_dir[1] + grad_x * light_dir[2])
    lighting = 0.3 + 0.7 * facing / jnp.sqrt(grad_sq + 1.0)
    sigma = jnp.zeros_like(values)
    bump_total = jnp.zeros_like(values)
    colour_red = jnp.zeros_like(values)
    colour_green = jnp.zeros_like(values)
    colour_blue = jnp.zeros_like(values)
    for bump_index in range(tf_centers.shape[0]):
        scaled = (values - tf_centers[bump_index]) / tf_widths[bump_index]
        bump = jnp.exp(-scaled * scaled)
        sigma = sigma + tf_density[bump_index] * bump
        bump_total = bump_total + bump
        colour_red = colour_red + tf_colors[0, bump_index] * bump
        colour_green = colour_green + tf_colors[1, bump_index] * bump
        colour_blue = colour_blue + tf_colors[2, bump_index] * bump
    factor = lighting / (bump_total + 0.1)
    emit = jnp.stack([colour_red * factor, colour_green * factor, colour_blue * factor], 0)
    depth_tau = sigma * (0.25 + grad_sq / (grad_sq + 1.0)) * step_size
    return (depth_tau, emit)

def compose_local(depth_tau, emit):
    before = jnp.cumsum(depth_tau, 0) - depth_tau
    weight_z = jnp.exp(-before) * (1.0 - jnp.exp(-depth_tau))
    colour_sum = lax.optimization_barrier(jnp.sum(weight_z[None] * emit, axis=1))
    return (colour_sum, lax.optimization_barrier(jnp.sum(depth_tau, 0)))

def reference(field, tf_centers, tf_widths, tf_density, tf_colors, light):
    padded = jnp.pad(field, 1)
    step_size = 0.5 / NZ
    band_count = NY // YD

    def one_band(band):
        start = (band * YD).astype(jnp.int32)
        piece = lax.dynamic_slice_in_dim(padded, start, YD + 2, 1).astype(jnp.float32)
        depth_tau, emit = shade_cells(piece, tf_centers, tf_widths, tf_density, tf_colors, light, step_size)
        colour_sum, tau_total = compose_local(depth_tau, emit)
        return jnp.concatenate([colour_sum, (1.0 - jnp.exp(-tau_total))[None]], 0)
    bands = lax.map(one_band, jnp.arange(band_count, dtype=jnp.int32))
    return jnp.transpose(bands, (1, 0, 2, 3)).reshape(4, NY, NX)
```

```python
import functools
import math

import jax
import jax.numpy as jnp
from jax import lax
from jax.experimental import pallas as pl
from jax.experimental.pallas import tpu as pltpu
from jax.sharding import PartitionSpec as P

MESH = pl.DeviceIdType.MESH
LANES = 128
SUB = 8
LAG = 8
WIDE = 2
DRAIN = 2
EARLY = 16
LOG2E = math.log2(math.e)
POWER = 8
RANGE = 11.0
DITHER = LOG2E / 1024 / POWER


def offset_of(group):
    return RANGE + group * DITHER


def encode(x, scale):
    y = x * scale
    for _ in range(POWER.bit_length() - 1):
        y = y * y
    return y


def decode(y, offset):
    return jnp.exp2(jnp.log2(y) * (1 / POWER) - offset)


def kernel(
    n, m, field, *rest,
):
    sources, image, tables = rest[:5], rest[5], rest[6:11]
    centers, widths, density, colors, light = tables
    (
        brick, halo_z, halo_y, cells, fixed, partial, held, packed, arrived, joined, kept, parts,
        table_sem, brick_sem, z_send, z_recv, y_send, y_recv, pair_send, pair_recv, own_send, own_recv,
    ) = rest[11:]
    planes, rows, columns = field.shape
    tiles = columns // LANES
    k = LANES * n // columns
    band_rows = SUB * k
    bands = rows // band_rows
    units = bands * tiles
    half = k // 2
    me = lax.axis_index("depth")
    row = lax.axis_index("rows")
    parity = lax.rem(me, 2)
    group = me // 2
    partner = me + 1 - 2 * parity
    last = n - 1

    barrier = pltpu.get_barrier_semaphore()

    def signal(where):
        pl.semaphore_signal(barrier, inc=1, device_id=where, device_id_type=MESH)

    load = pltpu.make_async_copy(field, brick, brick_sem)
    load.start()
    table_loads = [
        pltpu.make_async_copy(source, table, table_sem.at[i])
        for i, (source, table) in enumerate(zip(sources, tables))
    ]
    for copy in table_loads:
        copy.start()

    @pl.when(me > 0)
    def _():
        signal({"depth": me - 1})

    @pl.when(me < last)
    def _():
        signal({"depth": me + 1})

    @pl.when(row > 0)
    def _():
        signal({"rows": row - 1})

    @pl.when(row < m - 1)
    def _():
        signal({"rows": row + 1})

    signal({"depth": partner})
    for step in range(1, n // 2):
        signal({"depth": lax.rem(group + step, n // 2) * 2 + parity})

    for copy in table_loads:
        copy.wait()
    load.wait()

    zero_row = jnp.zeros((cells.shape[2], LANES), jnp.float32)

    def widen(z, carry):
        for t in range(tiles):
            cells[z, 1 + t, SUB : SUB + rows, :] = brick[
                z, :, t * LANES : (t + 1) * LANES
            ].astype(jnp.float32)
        cells[z, 0] = zero_row
        cells[z, tiles + 1] = zero_row
        return carry

    lax.fori_loop(0, planes, widen, 0)

    def band_of(i):
        return lax.rem(i + 1, bands)

    def z_copy(b, side):
        span = pl.ds(pl.multiple_of(b * band_rows, band_rows), band_rows)
        source = planes - 1 if side == 0 else 0
        where = me + 1 if side == 0 else me - 1
        return pltpu.make_async_remote_copy(
            src_ref=field.at[source, span],
            dst_ref=halo_z.at[side, span],
            send_sem=z_send.at[side],
            recv_sem=z_recv.at[side, b],
            device_id={"depth": where},
            device_id_type=MESH,
        )

    def y_copy(side):
        start = rows - SUB if side == 0 else 0
        where = row + 1 if side == 0 else row - 1
        return pltpu.make_async_remote_copy(
            src_ref=field.at[:, pl.ds(start, SUB)],
            dst_ref=halo_y.at[side],
            send_sem=y_send.at[side],
            recv_sem=y_recv.at[side],
            device_id={"rows": where},
            device_id_type=MESH,
        )

    has_source = (me > 0, me < last)
    has_target = (me < last, me > 0)
    row_source = (row > 0, row < m - 1)
    row_target = (row < m - 1, row > 0)

    for side in range(2):
        @pl.when(jnp.logical_not(has_source[side]))
        def _(side=side):
            halo_z[side] = jnp.zeros(halo_z.shape[1:], halo_z.dtype)

    def start_halos():
        expected = (
            (me > 0).astype(jnp.int32) + (me < last).astype(jnp.int32)
            + (row > 0).astype(jnp.int32) + (row < m - 1).astype(jnp.int32)
            + n // 2
        )
        pl.semaphore_wait(barrier, expected)
        for side in range(2):
            @pl.when(has_target[side])
            def _(side=side):
                def send(i, carry):
                    z_copy(band_of(i), side).start()
                    return carry

                lax.fori_loop(0, bands, send, 0)

        for side in range(2):
            @pl.when(row_target[side])
            def _(side=side):
                y_copy(side).start()

    def full(value):
        return jnp.full((SUB, LANES), value, jnp.float32)

    bumps = centers.shape[0]
    step_size = 0.5 / (planes * n)
    for i in range(bumps):
        w = full(widths[i])
        fixed[i] = full(centers[i])
        fixed[bumps + i] = -LOG2E / (w * w)
        fixed[2 * bumps + i] = full(density[i] * (-LOG2E * step_size * 4.0))
    axes = [full(light[i]) for i in range(3)]
    scale = 0.7 / jnp.sqrt(axes[0] * axes[0] + axes[1] * axes[1] + axes[2] * axes[2])
    for i in range(3):
        fixed[3 * bumps + i] = axes[i] * scale
    lane = lax.broadcasted_iota(jnp.int32, (SUB, LANES), 1)
    first_lane = lane == 0
    last_lane = lane == LANES - 1
    cell_shape = (k, SUB, LANES)
    offset = full(offset_of(group.astype(jnp.float32)))[:1]
    scale_up = jnp.exp2(offset)
    small = lax.broadcasted_iota(jnp.int32, (SUB, LANES), 1)

    def bump_sum(weights, values):
        total = weights[0] * values[0]
        for w, v in zip(weights[1:], values[1:]):
            total = total + w * v
        return total

    def place(s):
        b = band_of(s // tiles)
        t = lax.rem(lax.rem(s, tiles) + 1 + me // k, tiles)
        return b, t

    def pair_copy(s):
        return pltpu.make_async_remote_copy(
            src_ref=packed.at[s, 1 - parity],
            dst_ref=arrived.at[s],
            send_sem=pair_send,
            recv_sem=pair_recv.at[s],
            device_id={"depth": partner},
            device_id_type=MESH,
        )

    def own_copy(s, i):
        b, t = place(s)
        return pltpu.make_async_remote_copy(
            src_ref=joined.at[s, i],
            dst_ref=parts.at[group, b],
            send_sem=own_send,
            recv_sem=own_recv,
            device_id={"depth": t * k + 2 * i + parity},
            device_id_type=MESH,
        )

    def wait_halos(s):
        b, t = place(s)

        @pl.when(lax.rem(s, tiles) == 0)
        def _():
            for side in range(2):
                @pl.when(has_source[side])
                def _(side=side):
                    z_copy(b, side).wait_recv()

        @pl.when(s == max(bands - 2, 0) * tiles)
        def _():
            for side in range(2):
                spot = 0 if side == 0 else SUB + rows

                @pl.when(row_source[side])
                def _(side=side, spot=spot):
                    y_copy(side).wait_recv()

                    def put(z, carry):
                        for t in range(tiles):
                            cells[z, 1 + t, spot : spot + SUB, :] = halo_y[
                                side, z, :, t * LANES : (t + 1) * LANES
                            ].astype(jnp.float32)
                        return carry

                    lax.fori_loop(0, planes, put, 0)

                @pl.when(jnp.logical_not(row_source[side]))
                def _(spot=spot):
                    def put(z, carry):
                        for t in range(tiles):
                            cells[z, 1 + t, spot : spot + SUB, :] = jnp.zeros(
                                (SUB, LANES), jnp.float32
                            )
                        return carry

                    lax.fori_loop(0, planes, put, 0)

    def shade(s, first, last):
        b, t = place(s)
        base = pl.multiple_of(b * band_rows, band_rows)
        span = pl.ds(base + SUB, band_rows)
        halo_span = pl.ds(base, band_rows)
        halo_columns = pl.ds(pl.multiple_of(t * LANES, LANES), LANES)
        if first:
            through = jnp.ones(cell_shape, jnp.float32)
            depth = jnp.zeros(cell_shape, jnp.float32)
            sums = [jnp.zeros(cell_shape, jnp.float32) for _ in range(bumps)]
        else:
            through, depth, *sums = [partial[s, i] for i in range(bumps + 2)]
        centre = [fixed[i] for i in range(bumps)]
        narrow = [fixed[bumps + i] for i in range(bumps)]
        dense = [fixed[2 * bumps + i] for i in range(bumps)]
        ray = [fixed[3 * bumps + i] for i in range(3)]

        def cell(z, tile, rows):
            return cells[z, tile, rows, :].reshape(cell_shape)

        def edge(side):
            values = halo_z[side, halo_span, halo_columns].astype(jnp.float32)
            return values.reshape(cell_shape)

        order = list(range(1, planes - 1)) if first else []
        for z in order + ([planes - 1, 0] if last else []):
            v = cell(z, 1 + t, span)
            if z == 0:
                before = edge(0)
            else:
                before = cell(z - 1, 1 + t, span)
            if z == planes - 1:
                after = edge(1)
            else:
                after = cell(z + 1, 1 + t, span)
            dz = after - before
            dy = (
                cell(z, 1 + t, pl.ds(base + SUB + 1, band_rows))
                - cell(z, 1 + t, pl.ds(base + SUB - 1, band_rows))
            )
            left = jnp.where(
                first_lane,
                pltpu.roll(cell(z, t, span), 1, 2),
                pltpu.roll(v, 1, 2),
            )
            right = jnp.where(
                last_lane,
                pltpu.roll(cell(z, 2 + t, span), LANES - 1, 2),
                pltpu.roll(v, LANES - 1, 2),
            )
            dx = right - left
            r = lax.rsqrt(dz * dz + dy * dy + (dx * dx + 4.0))
            facing = jnp.abs(dz * ray[0] + dy * ray[1] + dx * ray[2])
            lighting = 0.3 + facing * r
            bump = []
            for i in range(bumps):
                u = v - centre[i]
                bump.append(jnp.exp2((u * u) * narrow[i]))
            tau = bump_sum(dense, bump) * (0.3125 - r * r)
            depth = depth + tau
            seen = jnp.exp2(tau)
            front = jnp.ones_like(seen) if z == 0 else through
            rest = front * seen
            inverse = lax.rsqrt((bump[0] + bump[1]) + (sum(bump[3:], bump[2]) + 0.1))
            weight = (front - rest) * lighting * (inverse * inverse)
            if z == 0:
                sums = [seen * total for total in sums]
            else:
                through = rest
            sums = [total + weight * value for total, value in zip(sums, bump)]
        if not last:
            for i, value in enumerate([through, depth] + sums):
                partial[s, i] = value
            return
        channels = [
            bump_sum([colors[c, i] for i in range(bumps)], sums) for c in range(3)
        ] + [-depth]
        codes = [[] for _ in range(k)]
        for c in range(4):
            blocks = [channels[c][i] for i in range(k)]
            for h in range(k):
                out = None
                for i in range(k):
                    shift = ((i - h) * LANES // k) % LANES
                    piece = pltpu.roll(blocks[i], shift, 1) if shift else blocks[i]
                    out = piece if i == 0 else jnp.where(small >= i * LANES // k, piece, out)
                held[s, h % 2, h // 2, c] = out
                codes[h].append(encode(out, scale_up))
        for h in range(k):
            for pair in range(2):
                packed[s, h % 2, h // 2, pair] = jnp.concatenate(
                    codes[h][2 * pair : 2 * pair + 2]
                ).astype(jnp.bfloat16)

    def merge(s):
        b, t = place(s)
        for i in range(half):
            mine = [held[s, parity, i, c] for c in range(4)]
            sent = [
                decode(arrived[s, i, pair].astype(jnp.float32), offset) for pair in range(2)
            ]
            other = [sent[c // 2][c % 2 * SUB : (c % 2 + 1) * SUB] for c in range(4)]
            front = parity == 0
            mine_scale = jnp.where(front, 1.0, jnp.exp2(-other[3]))
            other_scale = jnp.where(front, jnp.exp2(-mine[3]), 1.0)
            both = [
                mine[c] * mine_scale + other[c] * other_scale for c in range(3)
            ] + [mine[3] + other[3]]
            for pair in range(2):
                code = jnp.concatenate(
                    [encode(both[2 * pair + c], scale_up) for c in range(2)]
                ).astype(jnp.bfloat16)
                kept[b, i, pair] = code
                joined[s, i, pair] = code

    def pass_on(s):
        b, t = place(s)
        for i in range(half):
            @pl.when(t * k + 2 * i + parity != me)
            def _(i=i):
                own_copy(s, i).start()

    early = min(EARLY, tiles * max(bands - 2, 0))
    early = early - early % (2 * WIDE)
    late = early // 2 if early else min(LAG, units)
    turn = early + late

    def inner(s, carry):
        shade(s, True, False)
        return carry

    def halos_for(s):
        @pl.when(jnp.logical_and(lax.rem(s, tiles) == 0, s > 0))
        def _():
            wait_halos(s)

    def outer(i, carry):
        first = i * WIDE
        for w in range(WIDE):
            halos_for(first + w)
        for w in range(WIDE):
            shade(first + w, False, True)
        for w in range(WIDE):
            pair_copy(first + w).start()
        return carry

    def step_with(merges):
        def step(s, carry):
            halos_for(s)
            ready = merges(s)
            for u in ready:
                pair_copy(u).wait_recv()
            for u in ready:
                merge(u)
            shade(s, True, True)
            pair_copy(s).start()
            for u in ready:
                pass_on(u)
            return carry

        return step

    def drain_from(first, width):
        def drain(i, carry):
            ready = [first + i * width + w for w in range(width)]
            for u in ready:
                pair_copy(u).wait_recv()
            for u in ready:
                merge(u)
            for u in ready:
                pass_on(u)
            return carry

        return drain

    start_halos()
    lax.fori_loop(0, early, inner, 0)
    wait_halos(0)
    lax.fori_loop(0, early // WIDE, outer, 0)
    if early:
        lax.fori_loop(
            early, turn, step_with(lambda s: [2 * (s - early), 2 * (s - early) + 1]), 0
        )
    else:
        lax.fori_loop(0, late, step_with(lambda s: []), 0)
    lax.fori_loop(turn, units, step_with(lambda s: [s - late]), 0)
    width = DRAIN if late % DRAIN == 0 else 1
    lax.fori_loop(0, late // width, drain_from(units - late, width), 0)

    everything = parts.at[pl.ds(0, n // 2 - 1)]
    all_parts = pltpu.make_async_remote_copy(
        src_ref=everything,
        dst_ref=everything,
        send_sem=own_send,
        recv_sem=own_recv,
        device_id={"depth": partner},
        device_id_type=MESH,
    )
    all_parts.wait_recv()
    for b in range(bands):
        parts[group, b] = kept[b, lax.rem(me, k) // 2]

    for b in range(bands):
        depth = jnp.zeros((SUB, LANES), jnp.float32)
        tint = [jnp.zeros((SUB, LANES), jnp.float32) for _ in range(3)]
        for q in range(n // 2):
            seen = jnp.exp2(-depth)
            sent = [
                decode(parts[q, b, pair].astype(jnp.float32), offset_of(q)) for pair in range(2)
            ]
            part = [sent[c // 2][c % 2 * SUB : (c % 2 + 1) * SUB] for c in range(4)]
            tint = [tint[c] + seen * part[c] for c in range(3)]
            depth = depth + part[3]
        result = tint + [1.0 - jnp.exp2(-depth)]
        for c in range(4):
            for i in range(k):
                shift = (-i * LANES // k) % LANES
                piece = pltpu.roll(result[c], shift, 1) if shift else result[c]
                start = b * band_rows + i * SUB
                image[c, start : start + SUB, :] = piece[:, : LANES // k]

    for side in range(2):
        @pl.when(has_target[side])
        def _(side=side):
            pltpu.make_async_remote_copy(
                src_ref=field.at[0],
                dst_ref=halo_z.at[side],
                send_sem=z_send.at[side],
                recv_sem=z_recv.at[side, 0],
                device_id={"depth": partner},
                device_id_type=MESH,
            ).wait_send()

        @pl.when(row_target[side])
        def _(side=side):
            y_copy(side).wait_send()

    pltpu.make_async_remote_copy(
        src_ref=arrived,
        dst_ref=arrived,
        send_sem=pair_send,
        recv_sem=pair_recv.at[0],
        device_id={"depth": partner},
        device_id_type=MESH,
    ).wait_send()
    all_parts.wait_send()


def solution(mesh):
    n, m = mesh.shape["depth"], mesh.shape["rows"]

    def shards(field, centers, widths, density, colors, light):
        planes, rows, columns = field.shape
        tiles = columns // LANES
        k = LANES * n // columns
        bands = rows // (SUB * k)
        units = bands * tiles
        half = k // 2
        block = (4, SUB, LANES)
        code = (2, 2 * SUB, LANES)
        vmem, dma = pltpu.VMEM, pltpu.SemaphoreType.DMA
        operands = (field, centers, widths, density, colors, light)
        return pl.pallas_call(
            functools.partial(kernel, n, m),
            out_shape=jax.ShapeDtypeStruct((4, rows, columns // n), jnp.float32),
            in_specs=[pl.BlockSpec(memory_space=pltpu.HBM)] * 6,
            out_specs=pl.BlockSpec(memory_space=pltpu.VMEM),
            scratch_shapes=[pltpu.SMEM(a.shape, a.dtype) for a in operands[1:]]
            + [
                vmem(field.shape, field.dtype),
                vmem((2, rows, columns), field.dtype),
                vmem((2, planes, SUB, columns), field.dtype),
                vmem((planes, tiles + 2, rows + 2 * SUB, LANES), jnp.float32),
                vmem((3 * centers.shape[0] + 3, SUB, LANES), jnp.float32),
                vmem(
                    (EARLY, centers.shape[0] + 2, k, SUB, LANES), jnp.float32
                ),
                vmem((units, 2, half) + block, jnp.float32),
                vmem((units, 2, half) + code, jnp.bfloat16),
                vmem((units, half) + code, jnp.bfloat16),
                vmem((units, half) + code, jnp.bfloat16),
                vmem((bands, half) + code, jnp.bfloat16),
                vmem((n // 2, bands) + code, jnp.bfloat16),
                dma((5,)),
                dma,
                dma((2,)),
                dma((2, bands)),
                dma((2,)),
                dma((2,)),
                dma,
                dma((units,)),
                dma,
                dma,
            ],
            compiler_params=pltpu.CompilerParams(
                collective_id=0, has_side_effects=True, vmem_limit_bytes=67043328
            ),
            name="raycast",
        )(*operands)

    placed = (P("depth", "rows", None), P(), P(), P(), P(), P())
    return jax.shard_map(
        shards, mesh=mesh, in_specs=placed, out_specs=P(None, "rows", "depth"), check_vma=False
    )
```

```python
import functools
import math

import jax
import jax.numpy as jnp
from jax import lax
from jax.experimental import pallas as pl
from jax.experimental.pallas import tpu as pltpu
from jax.sharding import PartitionSpec as P

MESH = pl.DeviceIdType.MESH
LANES = 128
SUB = 8
LAG = 8
WIDE = 2
DRAIN = 4
RATE = 2
EARLY = 22
LOG2E = math.log2(math.e)
POWER = 8
RANGE = 11.0
DITHER = LOG2E / 1024 / POWER


def offset_of(group):
    return RANGE + group * DITHER


def encode(x, scale):
    y = x * scale
    for _ in range(POWER.bit_length() - 1):
        y = y * y
    return y


def decode(y, offset):
    return jnp.exp2(jnp.log2(y) * (1 / POWER) - offset)


def kernel(
    n, m, field, *rest,
):
    sources, image, tables = rest[:5], rest[5], rest[6:11]
    centers, widths, density, colors, light = tables
    (
        brick, halo_z, halo_y, cells, fixed, partial, held, packed, arrived, joined, kept, parts,
        table_sem, brick_sem, z_send, z_recv, y_send, y_recv, pair_send, pair_recv, own_send, own_recv,
    ) = rest[11:]
    planes, rows, columns = field.shape
    tiles = columns // LANES
    k = LANES * n // columns
    band_rows = SUB * k
    bands = rows // band_rows
    units = bands * tiles
    half = k // 2
    me = lax.axis_index("depth")
    row = lax.axis_index("rows")
    parity = lax.rem(me, 2)
    group = me // 2
    partner = me + 1 - 2 * parity
    last = n - 1

    barrier = pltpu.get_barrier_semaphore()

    def signal(where):
        pl.semaphore_signal(barrier, inc=1, device_id=where, device_id_type=MESH)

    load = pltpu.make_async_copy(field, brick, brick_sem)
    load.start()
    table_loads = [
        pltpu.make_async_copy(source, table, table_sem.at[i])
        for i, (source, table) in enumerate(zip(sources, tables))
    ]
    for copy in table_loads:
        copy.start()

    @pl.when(me > 0)
    def _():
        signal({"depth": me - 1})

    @pl.when(me < last)
    def _():
        signal({"depth": me + 1})

    @pl.when(row > 0)
    def _():
        signal({"rows": row - 1})

    @pl.when(row < m - 1)
    def _():
        signal({"rows": row + 1})

    signal({"depth": partner})
    for step in range(1, n // 2):
        signal({"depth": lax.rem(group + step, n // 2) * 2 + parity})

    for copy in table_loads:
        copy.wait()
    load.wait()

    zero_row = jnp.zeros((cells.shape[2], LANES), jnp.float32)

    def widen(z, carry):
        for t in range(tiles):
            cells[z, 1 + t, SUB : SUB + rows, :] = brick[
                z, :, t * LANES : (t + 1) * LANES
            ].astype(jnp.float32)
        cells[z, 0] = zero_row
        cells[z, tiles + 1] = zero_row
        return carry

    lax.fori_loop(0, planes, widen, 0)

    def band_of(i):
        return lax.rem(i + 1, bands)

    def z_copy(b, side):
        span = pl.ds(pl.multiple_of(b * band_rows, band_rows), band_rows)
        source = planes - 1 if side == 0 else 0
        where = me + 1 if side == 0 else me - 1
        return pltpu.make_async_remote_copy(
            src_ref=field.at[source, span],
            dst_ref=halo_z.at[side, span],
            send_sem=z_send.at[side],
            recv_sem=z_recv.at[side, b],
            device_id={"depth": where},
            device_id_type=MESH,
        )

    def y_copy(side):
        start = rows - SUB if side == 0 else 0
        where = row + 1 if side == 0 else row - 1
        return pltpu.make_async_remote_copy(
            src_ref=field.at[:, pl.ds(start, SUB)],
            dst_ref=halo_y.at[side],
            send_sem=y_send.at[side],
            recv_sem=y_recv.at[side],
            device_id={"rows": where},
            device_id_type=MESH,
        )

    has_source = (me > 0, me < last)
    has_target = (me < last, me > 0)
    row_source = (row > 0, row < m - 1)
    row_target = (row < m - 1, row > 0)

    for side in range(2):
        @pl.when(jnp.logical_not(has_source[side]))
        def _(side=side):
            halo_z[side] = jnp.zeros(halo_z.shape[1:], halo_z.dtype)

    def start_halos():
        expected = (
            (me > 0).astype(jnp.int32) + (me < last).astype(jnp.int32)
            + (row > 0).astype(jnp.int32) + (row < m - 1).astype(jnp.int32)
            + n // 2
        )
        pl.semaphore_wait(barrier, expected)
        def send(i, carry):
            for side in range(2):
                @pl.when(has_target[side])
                def _(side=side):
                    z_copy(band_of(i), side).start()

            return carry

        lax.fori_loop(0, bands, send, 0)
        for side in range(2):
            @pl.when(row_target[side])
            def _(side=side):
                y_copy(side).start()

    def full(value):
        return jnp.full((SUB, LANES), value, jnp.float32)

    bumps = centers.shape[0]
    step_size = 0.5 / (planes * n)
    for i in range(bumps):
        w = full(widths[i])
        fixed[i] = full(centers[i])
        fixed[bumps + i] = -LOG2E / (w * w)
        fixed[2 * bumps + i] = full(density[i] * (-LOG2E * step_size * 4.0))
    axes = [full(light[i]) for i in range(3)]
    scale = 0.7 / jnp.sqrt(axes[0] * axes[0] + axes[1] * axes[1] + axes[2] * axes[2])
    for i in range(3):
        fixed[3 * bumps + i] = axes[i] * scale
    lane = lax.broadcasted_iota(jnp.int32, (SUB, LANES), 1)
    first_lane = lane == 0
    last_lane = lane == LANES - 1
    cell_shape = (k, SUB, LANES)
    offset = full(offset_of(group.astype(jnp.float32)))[:1]
    scale_up = jnp.exp2(offset)
    small = lax.broadcasted_iota(jnp.int32, (SUB, LANES), 1)

    def bump_sum(weights, values):
        total = weights[0] * values[0]
        for w, v in zip(weights[1:], values[1:]):
            total = total + w * v
        return total

    def place(s):
        b = band_of(s // tiles)
        t = lax.rem(lax.rem(s, tiles) + 1 + me // k, tiles)
        return b, t

    def pair_copy(s):
        return pltpu.make_async_remote_copy(
            src_ref=packed.at[s, 1 - parity],
            dst_ref=arrived.at[s],
            send_sem=pair_send,
            recv_sem=pair_recv.at[s],
            device_id={"depth": partner},
            device_id_type=MESH,
        )

    def own_copy(s, i):
        b, t = place(s)
        return pltpu.make_async_remote_copy(
            src_ref=joined.at[s, i],
            dst_ref=parts.at[group, b],
            send_sem=own_send,
            recv_sem=own_recv,
            device_id={"depth": t * k + 2 * i + parity},
            device_id_type=MESH,
        )

    def wait_halos(s):
        b, t = place(s)

        @pl.when(lax.rem(s, tiles) == 0)
        def _():
            for side in range(2):
                @pl.when(has_source[side])
                def _(side=side):
                    z_copy(b, side).wait_recv()

    def wait_rows(s):
        @pl.when(s == max(bands - 2, 0) * tiles)
        def _():
            for side in range(2):
                spot = 0 if side == 0 else SUB + rows

                @pl.when(row_source[side])
                def _(side=side, spot=spot):
                    y_copy(side).wait_recv()

                    def put(z, carry):
                        for t in range(tiles):
                            cells[z, 1 + t, spot : spot + SUB, :] = halo_y[
                                side, z, :, t * LANES : (t + 1) * LANES
                            ].astype(jnp.float32)
                        return carry

                    lax.fori_loop(0, planes, put, 0)

                @pl.when(jnp.logical_not(row_source[side]))
                def _(spot=spot):
                    def put(z, carry):
                        for t in range(tiles):
                            cells[z, 1 + t, spot : spot + SUB, :] = jnp.zeros(
                                (SUB, LANES), jnp.float32
                            )
                        return carry

                    lax.fori_loop(0, planes, put, 0)

    def shade(s, first, last):
        b, t = place(s)
        base = pl.multiple_of(b * band_rows, band_rows)
        span = pl.ds(base + SUB, band_rows)
        halo_span = pl.ds(base, band_rows)
        halo_columns = pl.ds(pl.multiple_of(t * LANES, LANES), LANES)
        if first:
            through = jnp.ones(cell_shape, jnp.float32)
            depth = jnp.zeros(cell_shape, jnp.float32)
            sums = [jnp.zeros(cell_shape, jnp.float32) for _ in range(bumps)]
        else:
            through, depth, *sums = [partial[s, i] for i in range(bumps + 2)]
        centre = [fixed[i] for i in range(bumps)]
        narrow = [fixed[bumps + i] for i in range(bumps)]
        dense = [fixed[2 * bumps + i] for i in range(bumps)]
        ray = [fixed[3 * bumps + i] for i in range(3)]

        def cell(z, tile, rows):
            return cells[z, tile, rows, :].reshape(cell_shape)

        def edge(side):
            values = halo_z[side, halo_span, halo_columns].astype(jnp.float32)
            return values.reshape(cell_shape)

        order = list(range(1, planes - 1)) if first else []
        for z in order + ([planes - 1, 0] if last else []):
            v = cell(z, 1 + t, span)
            if z == 0:
                before = edge(0)
            else:
                before = cell(z - 1, 1 + t, span)
            if z == planes - 1:
                after = edge(1)
            else:
                after = cell(z + 1, 1 + t, span)
            dz = after - before
            dy = (
                cell(z, 1 + t, pl.ds(base + SUB + 1, band_rows))
                - cell(z, 1 + t, pl.ds(base + SUB - 1, band_rows))
            )
            left = jnp.where(
                first_lane,
                pltpu.roll(cell(z, t, span), 1, 2),
                pltpu.roll(v, 1, 2),
            )
            right = jnp.where(
                last_lane,
                pltpu.roll(cell(z, 2 + t, span), LANES - 1, 2),
                pltpu.roll(v, LANES - 1, 2),
            )
            dx = right - left
            r = lax.rsqrt(dz * dz + dy * dy + (dx * dx + 4.0))
            facing = jnp.abs(dz * ray[0] + dy * ray[1] + dx * ray[2])
            lighting = 0.3 + facing * r
            bump = []
            for i in range(bumps):
                u = v - centre[i]
                bump.append(jnp.exp2((u * u) * narrow[i]))
            tau = bump_sum(dense, bump) * (0.3125 - r * r)
            depth = depth + tau
            seen = jnp.exp2(tau)
            front = jnp.ones_like(seen) if z == 0 else through
            rest = front * seen
            inverse = lax.rsqrt((bump[0] + bump[1]) + (sum(bump[3:], bump[2]) + 0.1))
            weight = (front - rest) * lighting * (inverse * inverse)
            if z == 0:
                sums = [seen * total for total in sums]
            else:
                through = rest
            sums = [total + weight * value for total, value in zip(sums, bump)]
        if not last:
            for i, value in enumerate([through, depth] + sums):
                partial[s, i] = value
            return
        channels = [
            bump_sum([colors[c, i] for i in range(bumps)], sums) for c in range(3)
        ] + [-depth]
        codes = [[] for _ in range(k)]
        for c in range(4):
            blocks = [channels[c][i] for i in range(k)]
            for h in range(k):
                out = None
                for i in range(k):
                    shift = ((i - h) * LANES // k) % LANES
                    piece = pltpu.roll(blocks[i], shift, 1) if shift else blocks[i]
                    out = piece if i == 0 else jnp.where(small >= i * LANES // k, piece, out)
                held[s, h % 2, h // 2, c] = out
                codes[h].append(encode(out, scale_up))
        for h in range(k):
            for pair in range(2):
                packed[s, h % 2, h // 2, pair] = jnp.concatenate(
                    codes[h][2 * pair : 2 * pair + 2]
                ).astype(jnp.bfloat16)

    def merge(s):
        b, t = place(s)
        for i in range(half):
            mine = [held[s, parity, i, c] for c in range(4)]
            sent = [
                decode(arrived[s, i, pair].astype(jnp.float32), offset) for pair in range(2)
            ]
            other = [sent[c // 2][c % 2 * SUB : (c % 2 + 1) * SUB] for c in range(4)]
            front = parity == 0
            mine_scale = jnp.where(front, 1.0, jnp.exp2(-other[3]))
            other_scale = jnp.where(front, jnp.exp2(-mine[3]), 1.0)
            both = [
                mine[c] * mine_scale + other[c] * other_scale for c in range(3)
            ] + [mine[3] + other[3]]
            for pair in range(2):
                code = jnp.concatenate(
                    [encode(both[2 * pair + c], scale_up) for c in range(2)]
                ).astype(jnp.bfloat16)
                kept[b, i, pair] = code
                joined[s, i, pair] = code

    def pass_on(s):
        b, t = place(s)
        for i in range(half):
            @pl.when(t * k + 2 * i + parity != me)
            def _(i=i):
                own_copy(s, i).start()

    early = min(EARLY, units) if bands > 2 else 0
    early = early - early % WIDE
    catch = min(early // RATE, units - early) if early else min(LAG, units)
    turn = early + catch
    late = turn - RATE * catch if early else catch
    edge = max(bands - 2, 0) * tiles

    def inner(s, carry):
        if edge < early:
            wait_rows(s)
        shade(s, True, False)
        return carry

    def halos_for(s):
        @pl.when(jnp.logical_and(lax.rem(s, tiles) == 0, s > 0))
        def _():
            wait_halos(s)

        if edge >= early:
            wait_rows(s)

    def outer(i, carry):
        first = i * WIDE
        for w in range(WIDE):
            halos_for(first + w)
        for w in range(WIDE):
            shade(first + w, False, True)
        for w in range(WIDE):
            pair_copy(first + w).start()
        return carry

    def step_with(merges):
        def step(s, carry):
            halos_for(s)
            ready = merges(s)
            for u in ready:
                pair_copy(u).wait_recv()
            for u in ready:
                merge(u)
            shade(s, True, True)
            pair_copy(s).start()
            for u in ready:
                pass_on(u)
            return carry

        return step

    def drain_from(first, width):
        def drain(i, carry):
            ready = [first + i * width + w for w in range(width)]
            for u in ready:
                pair_copy(u).wait_recv()
            for u in ready:
                merge(u)
            for u in ready:
                pass_on(u)
            return carry

        return drain

    start_halos()
    lax.fori_loop(0, early, inner, 0)
    wait_halos(0)
    lax.fori_loop(0, early // WIDE, outer, 0)
    if early:
        lax.fori_loop(
            early, turn, step_with(lambda s: [RATE * (s - early) + r for r in range(RATE)]), 0
        )
    else:
        lax.fori_loop(0, turn, step_with(lambda s: []), 0)
    lax.fori_loop(turn, units, step_with(lambda s: [s - late]), 0)
    width = DRAIN if late % DRAIN == 0 else 1
    lax.fori_loop(0, late // width, drain_from(units - late, width), 0)

    everything = parts.at[pl.ds(0, n // 2 - 1)]
    all_parts = pltpu.make_async_remote_copy(
        src_ref=everything,
        dst_ref=everything,
        send_sem=own_send,
        recv_sem=own_recv,
        device_id={"depth": partner},
        device_id_type=MESH,
    )
    all_parts.wait_recv()
    for b in range(bands):
        parts[group, b] = kept[b, lax.rem(me, k) // 2]

    for b in range(bands):
        depth = jnp.zeros((SUB, LANES), jnp.float32)
        tint = [jnp.zeros((SUB, LANES), jnp.float32) for _ in range(3)]
        for q in range(n // 2):
            seen = jnp.exp2(-depth)
            sent = [
                decode(parts[q, b, pair].astype(jnp.float32), offset_of(q)) for pair in range(2)
            ]
            part = [sent[c // 2][c % 2 * SUB : (c % 2 + 1) * SUB] for c in range(4)]
            tint = [tint[c] + seen * part[c] for c in range(3)]
            depth = depth + part[3]
        result = tint + [1.0 - jnp.exp2(-depth)]
        for c in range(4):
            for i in range(k):
                shift = (-i * LANES // k) % LANES
                piece = pltpu.roll(result[c], shift, 1) if shift else result[c]
                start = b * band_rows + i * SUB
                image[c, start : start + SUB, :] = piece[:, : LANES // k]

    for side in range(2):
        @pl.when(has_target[side])
        def _(side=side):
            pltpu.make_async_remote_copy(
                src_ref=field.at[0],
                dst_ref=halo_z.at[side],
                send_sem=z_send.at[side],
                recv_sem=z_recv.at[side, 0],
                device_id={"depth": partner},
                device_id_type=MESH,
            ).wait_send()

        @pl.when(row_target[side])
        def _(side=side):
            y_copy(side).wait_send()

    pltpu.make_async_remote_copy(
        src_ref=arrived,
        dst_ref=arrived,
        send_sem=pair_send,
        recv_sem=pair_recv.at[0],
        device_id={"depth": partner},
        device_id_type=MESH,
    ).wait_send()
    all_parts.wait_send()


def solution(mesh):
    n, m = mesh.shape["depth"], mesh.shape["rows"]

    def shards(field, centers, widths, density, colors, light):
        planes, rows, columns = field.shape
        tiles = columns // LANES
        k = LANES * n // columns
        bands = rows // (SUB * k)
        units = bands * tiles
        half = k // 2
        block = (4, SUB, LANES)
        code = (2, 2 * SUB, LANES)
        vmem, dma = pltpu.VMEM, pltpu.SemaphoreType.DMA
        operands = (field, centers, widths, density, colors, light)
        return pl.pallas_call(
            functools.partial(kernel, n, m),
            out_shape=jax.ShapeDtypeStruct((4, rows, columns // n), jnp.float32),
            in_specs=[pl.BlockSpec(memory_space=pltpu.HBM)] * 6,
            out_specs=pl.BlockSpec(memory_space=pltpu.VMEM),
            scratch_shapes=[pltpu.SMEM(a.shape, a.dtype) for a in operands[1:]]
            + [
                vmem(field.shape, field.dtype),
                vmem((2, rows, columns), field.dtype),
                vmem((2, planes, SUB, columns), field.dtype),
                vmem((planes, tiles + 2, rows + 2 * SUB, LANES), jnp.float32),
                vmem((3 * centers.shape[0] + 3, SUB, LANES), jnp.float32),
                vmem(
                    (EARLY, centers.shape[0] + 2, k, SUB, LANES), jnp.float32
                ),
                vmem((units, 2, half) + block, jnp.float32),
                vmem((units, 2, half) + code, jnp.bfloat16),
                vmem((units, half) + code, jnp.bfloat16),
                vmem((units, half) + code, jnp.bfloat16),
                vmem((bands, half) + code, jnp.bfloat16),
                vmem((n // 2, bands) + code, jnp.bfloat16),
                dma((5,)),
                dma,
                dma((2,)),
                dma((2, bands)),
                dma((2,)),
                dma((2,)),
                dma,
                dma((units,)),
                dma,
                dma,
            ],
            compiler_params=pltpu.CompilerParams(
                collective_id=0, has_side_effects=True, vmem_limit_bytes=67043328
            ),
            name="raycast",
        )(*operands)

    placed = (P("depth", "rows", None), P(), P(), P(), P(), P())
    return jax.shard_map(
        shards, mesh=mesh, in_specs=placed, out_specs=P(None, "rows", "depth"), check_vma=False
    )
```
